256 devices in a mesh: section: 2 (over core), dom: 128 (over x, z, y).
Axes of the slice: x: 4, y: 4, z: 8, core: 2. Of those that a mesh axis runs over, the one named last changes fastest.
Arguments:
- node_feats: bfloat16 [2, 32768, 512], P(None, 'dom'), may hold values from -6 to 6
- edge_feats: bfloat16 [2, 65536, 512], P(None, 'dom'), may hold values from -6 to 6
- edge_src: int32 [65536], P('dom'), may hold values from 0 to 511, as said below
- edge_dst: int32 [65536], P('dom'), may hold values from 0 to 255
- edge_count: int32 [128], P('dom'), may hold values from 256 to 512, as said below
- send_rows: int32 [16384, 2], P('dom'), may hold values from 0 to 255
- edge_w1: bfloat16 [2, 3, 512, 512], P('section'), may hold values from -0.15625 to 0.15625
- edge_b1: bfloat16 [2, 512], P('section'), may hold values from -3 to 3
- edge_w2: bfloat16 [2, 512, 512], P('section'), may hold values from -0.25 to 0.25
- edge_gain: bfloat16 [2, 512], P('section'), may hold values from 0.5 to 1.5
- node_w1: bfloat16 [2, 2, 512, 512], P('section'), may hold values from -0.1875 to 0.1875
- node_b1: bfloat16 [2, 512], P('section'), may hold values from -3 to 3
- node_w2: bfloat16 [2, 512, 512], P('section'), may hold values from -0.25 to 0.25
- node_gain: bfloat16 [2, 512], P('section'), may hold values from 0.5 to 1.5
Outputs:
- node_out: bfloat16 [2, 2, 32768, 512], P('section', None, 'dom')
- edge_out: bfloat16 [2, 2, 65536, 512], P('section', None, 'dom')
The draws below stay inside these ranges and needn't reach their ends.
Inputs may be any that keep to these rules, and one draw needn't show every extreme that they name: `edge_src`: among a device's 512 slots, the first 256 name each value from 256 upward exactly once; the others are below 256. `edge_count`: some device has all 512 slots live.
All inputs are finite; a program needn't handle non-finite values.
Results may differ from the reference program's by a relative error of at most 0.0065.
Values may be sent and summed in bfloat16 or wider, within the bound.
No kernel may reach another device: no remote copies, remote signals or barrier semaphores. Data moves between devices by JAX's collectives and lax.ppermute only.
A program may use at most 64 MiB of HBM per device.

```python
import jax
import jax.numpy as jnp
from jax import lax

D = 512
H = 512
NODE_DEV = 256
EDGE_DEV = 512
HCAP = 2
MB = 2
LAYERS = 2
PEERS = 128
NODES = 32768
EDGES = 65536


def draw_edge_src(key, part):
    key_list = jax.random.split(key, PEERS)
    halo_slots = jax.vmap(lambda single: jax.random.permutation(single, PEERS * HCAP))(key_list) + NODE_DEV
    local_rows = jax.random.randint(jax.random.fold_in(key, 7), (PEERS, EDGE_DEV - PEERS * HCAP), 0, NODE_DEV)
    return jnp.concatenate([halo_slots.astype(jnp.int32), local_rows.astype(jnp.int32)], axis=1).reshape(-1)


def draw_edge_count(key, part):
    counts = jax.random.randint(key, (PEERS,), EDGE_DEV // 2, EDGE_DEV + 1)
    fullest = jax.random.randint(jax.random.fold_in(key, 11), (), 0, PEERS)
    return counts.at[fullest].set(EDGE_DEV).astype(jnp.int32)


def plant(result, key, smallest, largest):
    longest = result.shape.index(max(result.shape))
    spots = []
    for shift in (0, 1):
        where = [jax.random.randint(jax.random.fold_in(key, axis), (), 0, length) for axis, length in enumerate(result.shape)]
        where[longest] = (where[longest] + shift) % result.shape[longest]
        spots.append(tuple(where))
    return result.at[spots[0]].set(smallest).at[spots[1]].set(largest)


def block_scale(key, shape, pieces, least, top_value):
    loudness, own = 1.0, jax.random.fold_in(key, 6)
    for axis_at, parts in pieces:
        draws = jnp.exp(jax.random.uniform(jax.random.fold_in(own, axis_at), (parts,), jnp.float32, least / len(pieces), top_value / len(pieces)))
        loudness = loudness * jnp.repeat(draws, shape[axis_at] // parts).reshape([-1 if axis == axis_at else 1 for axis in range(len(shape))])
    return loudness


def gaussian(rng, extent, deviation, bound, cuts=(), kind=jnp.bfloat16):
    result = jax.random.normal(rng, extent, jnp.float32) * deviation
    if len(cuts) > 0:
        result = block_scale(rng, extent, cuts, -0.22, 0.18) * result
    return jnp.clip(result, min=-bound, max=bound).astype(kind)


def setup_inputs(seed: int = 0) -> dict:
    splits = jax.random.split(jax.random.key(seed), 15)
    node_feats = gaussian(splits[0], (MB, NODES, D), 1.0, 6.0, ((1, 128),))
    edge_feats = gaussian(splits[1], (MB, EDGES, D), 1.0, 6.0, ((1, 128),))
    edge_src = draw_edge_src(jax.random.fold_in(splits[14], 71), 0)
    edge_dst = plant(jax.random.randint(splits[3], (EDGES,), 0, NODE_DEV), jax.random.fold_in(splits[3], 1), 0, NODE_DEV - 1).astype(jnp.int32)
    edge_count = draw_edge_count(jax.random.fold_in(splits[14], 71), 0)
    send_rows = plant(jax.random.randint(splits[5], (PEERS * PEERS, HCAP), 0, NODE_DEV), jax.random.fold_in(splits[5], 1), 0, NODE_DEV - 1).astype(jnp.int32)
    edge_w1 = gaussian(splits[6], (LAYERS, 3, D, H), (3 * D) ** -0.5, 0.15625, ((0, 2),))
    edge_b1 = gaussian(splits[7], (LAYERS, H), 0.5, 3.0, ((0, 2),))
    edge_w2 = gaussian(splits[8], (LAYERS, H, D), H ** -0.5, 0.25, ((0, 2),))
    edge_gain = jnp.clip(1.0 + 0.1 * jax.random.normal(splits[9], (LAYERS, D), jnp.float32), 0.5, 1.5).astype(jnp.bfloat16)
    node_w1 = gaussian(splits[10], (LAYERS, 2, D, H), (2 * D) ** -0.5, 0.1875, ((0, 2),))
    node_b1 = gaussian(splits[11], (LAYERS, H), 0.5, 3.0, ((0, 2),))
    node_w2 = gaussian(splits[12], (LAYERS, H, D), H ** -0.5, 0.25, ((0, 2),))
    node_gain = jnp.clip(1.0 + 0.1 * jax.random.normal(splits[13], (LAYERS, D), jnp.float32), 0.5, 1.5).astype(jnp.bfloat16)
    return dict(node_feats=node_feats, edge_feats=edge_feats, edge_src=edge_src, edge_dst=edge_dst, edge_count=edge_count, send_rows=send_rows, edge_w1=edge_w1, edge_b1=edge_b1, edge_w2=edge_w2, edge_gain=edge_gain, node_w1=node_w1, node_b1=node_b1, node_w2=node_w2, node_gain=node_gain)


def layer_norm(values, gain):
    row_mean = lax.optimization_barrier(jnp.mean(values, axis=-1, keepdims=True))
    centred = values - row_mean
    row_var = lax.optimization_barrier(jnp.mean(centred * centred, axis=-1, keepdims=True))
    return centred * lax.rsqrt(row_var + 1e-05) * gain.astype(jnp.float32)

def apply_layer(node_lat, edge_lat, weights, sender, receiver, live_mask):
    edge_w1, edge_b1, edge_w2, edge_gain, node_w1, node_b1, node_w2, node_gain = weights
    from_sender = jnp.dot(node_lat, edge_w1[1], preferred_element_type=jnp.float32)
    from_receiver = jnp.dot(node_lat, edge_w1[2], preferred_element_type=jnp.float32)

    def one_device(items):
        block_edges, block_sender, block_receiver, block_live = items
        hidden = jnp.dot(block_edges, edge_w1[0], preferred_element_type=jnp.float32)
        hidden = hidden + from_sender[block_sender] + from_receiver[block_receiver] + edge_b1.astype(jnp.float32)
        hidden = jax.nn.silu(hidden).astype(jnp.bfloat16)
        update = layer_norm(jnp.dot(hidden, edge_w2, preferred_element_type=jnp.float32), edge_gain)
        update = update * block_live[:, None]
        new_edges = (block_edges.astype(jnp.float32) + update).astype(jnp.bfloat16)
        return (new_edges, update.astype(jnp.bfloat16))
    new_edges, message = lax.map(one_device, (edge_lat.reshape(PEERS, EDGE_DEV, D), sender, receiver, live_mask))
    incoming = jax.ops.segment_sum(message.reshape(-1, D).astype(jnp.float32), receiver.reshape(-1), num_segments=NODES)
    incoming = incoming.astype(jnp.bfloat16)
    node_hidden = jnp.dot(node_lat, node_w1[0], preferred_element_type=jnp.float32)
    node_hidden = node_hidden + jnp.dot(incoming, node_w1[1], preferred_element_type=jnp.float32) + node_b1.astype(jnp.float32)
    node_hidden = jax.nn.silu(node_hidden).astype(jnp.bfloat16)
    node_update = layer_norm(jnp.dot(node_hidden, node_w2, preferred_element_type=jnp.float32), node_gain)
    new_nodes = (node_lat.astype(jnp.float32) + node_update).astype(jnp.bfloat16)
    return (new_nodes, new_edges.reshape(-1, D))

def reference(node_feats, edge_feats, edge_src, edge_dst, edge_count, send_rows, edge_w1, edge_b1, edge_w2, edge_gain, node_w1, node_b1, node_w2, node_gain):
    source = edge_src.reshape(PEERS, EDGE_DEV)
    target = edge_dst.reshape(PEERS, EDGE_DEV)
    owner_dev = jnp.arange(PEERS, dtype=jnp.int32)[:, None]
    halo_slot = jnp.clip(source - NODE_DEV, 0, PEERS * HCAP - 1).astype(jnp.int32)
    peer_dev = halo_slot // HCAP
    slot_part = halo_slot % HCAP
    remote = peer_dev * NODE_DEV + send_rows[peer_dev * PEERS + owner_dev, slot_part]
    sender = jnp.where(source < NODE_DEV, owner_dev * NODE_DEV + source, remote).astype(jnp.int32)
    receiver = (owner_dev * NODE_DEV + target).astype(jnp.int32)
    positions = jnp.arange(EDGE_DEV, dtype=jnp.int32)[None, :]
    live_mask = (positions < edge_count[:, None]).astype(jnp.float32)
    node_layers = []
    edge_layers = []
    current_nodes = [node_feats[batch_num] for batch_num in range(MB)]
    current_edges = [edge_feats[batch_num] for batch_num in range(MB)]
    for layer_num in range(LAYERS):
        weights = (edge_w1[layer_num], edge_b1[layer_num], edge_w2[layer_num], edge_gain[layer_num], node_w1[layer_num], node_b1[layer_num], node_w2[layer_num], node_gain[layer_num])
        for batch_num in range(MB):
            current_nodes[batch_num], current_edges[batch_num] = apply_layer(current_nodes[batch_num], current_edges[batch_num], weights, sender, receiver, live_mask)
        node_layers.append(jnp.stack(current_nodes))
        edge_layers.append(jnp.stack(current_edges))
    return (jnp.stack(node_layers), jnp.stack(edge_layers))
```

```python
import functools

import jax
import jax.numpy as jnp
from jax import lax
from jax.experimental import pallas as pl
from jax.experimental.pallas import tpu as pltpu
from jax.sharding import PartitionSpec as P


F32 = jnp.float32
BF16 = jnp.bfloat16
VMEM = pl.BlockSpec(memory_space=pltpu.VMEM)
SMEM = pl.BlockSpec(memory_space=pltpu.SMEM)
ANY = pl.BlockSpec(memory_space=pl.ANY)
LIMIT = 67043328


def dot(a, b):
    return jnp.dot(a, b, preferred_element_type=F32)


def dot_ta(a, b):
    return lax.dot_general(a, b, (((0,), (0,)), ((), ())), preferred_element_type=F32)


def dot_tb(a, b):
    return lax.dot_general(a, b, (((1,), (1,)), ((), ())), preferred_element_type=F32)


def silu(x):
    half = 0.5 * x
    return half + half * jnp.tanh(half)


def centre(y):
    c = y - jnp.mean(y, axis=-1, keepdims=True)
    var = jnp.mean(c * c, axis=-1, keepdims=True)
    return c * lax.rsqrt(var + 1e-05)


def pick_onehot(row, ids):
    return (ids == row).astype(F32).astype(BF16)


def sublane_ids(rows, cols):
    return lax.broadcasted_iota(jnp.int32, (rows, cols), 0)


def arrival_ids(half, peers, first):
    q = sublane_ids(half, half)
    return first + (half // peers) * (q % peers) + q // peers


def send_onehot(idx, nodes):
    row = jnp.concatenate([idx[k : k + 1] for k in range(idx.shape[0])], axis=1)
    return pick_onehot(row, sublane_ids(nodes, row.shape[1]))


def pack_rows(picked, msg, tmp, peers):
    per, lanes = picked.shape[0] // peers, picked.shape[1] // 128
    for k in range(per):
        for c in range(lanes):
            tmp[pl.ds(k * lanes + c, peers, stride=per * lanes), :] = (
                picked[k * peers : (k + 1) * peers, c * 128 : (c + 1) * 128])
    msg[...] = tmp[...].astype(BF16)


def unpack_rows(msg, tmp, half, width, peers):
    per, lanes = half // peers, width // 128
    tmp[...] = msg[...].astype(F32)
    blocks = [
        jnp.concatenate(
            [tmp[pl.ds(k * lanes + c, peers, stride=per * lanes), :] for c in range(lanes)], axis=1)
        for k in range(per)
    ]
    return jnp.concatenate(blocks, axis=0).astype(BF16)


def start(pairs, sems):
    copies = [pltpu.make_async_copy(a, b, sems.at[i]) for i, (a, b) in enumerate(pairs)]
    for c in copies:
        c.start()
    return copies


def wait(copies):
    for c in copies:
        c.wait()


def matrices(refs):
    ew1, ew2, nw1, nw2 = refs
    return ew1.at[0, 0], ew1.at[0, 1], ew1.at[0, 2], ew2.at[0], nw1.at[0, 0], nw1.at[0, 1], nw2.at[0]


def fetch_weights(mine, own, oth, which, w, sems):
    @pl.when(mine)
    def _():
        start([(matrices(own)[k], w.at[i]) for i, k in enumerate(which)], sems)

    @pl.when(jnp.logical_not(mine))
    def _():
        start([(matrices(oth)[k], w.at[i]) for i, k in enumerate(which)], sems)

    return [pltpu.make_async_copy(matrices(own)[k], w.at[i], sems.at[i]) for i, k in enumerate(which)]


LOCAL = (0, 1, 2, 3, 4)
FINISH = (1, 3, 5, 6)


def select_kernel(peers, sec, idx_h, feats, msg_h, idx, lat, msg, tmp, sems):
    c_idx, c_lat = start(((idx_h, idx), (feats.at[sec[0]], lat)), sems)
    c_idx.wait()
    oh = send_onehot(idx[...], lat.shape[0])
    c_lat.wait()
    pack_rows(dot_ta(oh, lat[...]), msg, tmp, peers)
    wait(start(((msg, msg_h),), sems))


def local_work(count, src, dst, v, e_halo, e_local, w, vec, oh_q, outs):
    pre_q, part, pre_n = outs
    half = src.shape[1] // 2
    nodes = v.shape[0]
    ids = sublane_ids(nodes, half)
    recv_l = pick_onehot(dst[:, half:], ids)
    send_l = pick_onehot(src[:, half:], ids)
    vs_l = dot_ta(send_l, v).astype(BF16)
    vr_l = dot_ta(recv_l, v).astype(BF16)
    vr_q = dot_ta(oh_q, v).astype(BF16)
    pre_q[...] = dot(e_halo, w[0]) + dot(vr_q, w[2]) + vec[0:1]
    h = dot(e_local, w[0]) + dot(vs_l, w[1]) + dot(vr_l, w[2]) + vec[0:1]
    y = centre(dot(silu(h).astype(BF16), w[3])) * vec[1:2]
    pos = sublane_ids(half, 1) + half
    upd = jnp.where(pos < count[0], y, 0.0)
    part[...] = dot(recv_l, upd.astype(BF16))
    pre_n[...] = dot(v, w[4]) + vec[2:3]
    return (e_local.astype(F32) + upd).astype(BF16)


def pick_vec(mine, vec_own, vec_oth):
    return jnp.where(mine, vec_own[...].astype(F32), vec_oth[...].astype(F32))


def first_local_kernel(peers, sec, count, src_h, dst_h, idx_h, nfeats, efeats, ew1, ew2, nw1, nw2,
                       xew1, xew2, xnw1, xnw2, vo_h, vx_h,
                       pre_q_h, part_h, pre_n_h, e1_loc_h, lat_h, e_q_h, oh_q_h, oh_s_h, perm_h, live_h,
                       src, dst, idx, vo, vx, lat, e, w, pre_q, part, pre_n, e1_loc, e_q, oh_q, oh_s, perm_q, live_q,
                       sem_w, sem_in, sem_out):
    half = src.shape[1] // 2
    nodes = lat.shape[0]
    mine = sec[0] == 0
    ins = start(((src_h, src), (dst_h, dst), (idx_h, idx), (efeats.at[sec[0]], e), (nfeats.at[sec[0]], lat),
                 (vo_h, vo), (vx_h, vx)), sem_in)
    weights = fetch_weights(mine, (ew1, ew2, nw1, nw2), (xew1, xew2, xnw1, xnw2), LOCAL, w, sem_w)
    wait(ins)
    oh_s[...] = send_onehot(idx[...], nodes)
    perm = pick_onehot(src[:, :half], arrival_ids(half, peers, nodes))
    perm_q[...] = perm
    recv_h = pick_onehot(dst[:, :half], sublane_ids(nodes, half))
    ohq = dot_tb(recv_h, perm).astype(BF16)
    oh_q[...] = ohq
    pos = lax.broadcasted_iota(jnp.int32, (half, half), 1)
    live = jnp.sum(jnp.where(pos < count[0], perm.astype(F32), 0.0), axis=1, keepdims=True)
    live_q[...] = jnp.broadcast_to(live, live_q.shape)
    eq = dot(perm, e[:half]).astype(BF16)
    e_q[...] = eq
    wait(weights)
    e1_loc[...] = local_work(count, src, dst, lat[...], eq, e[half:], w, pick_vec(mine, vo, vx), ohq,
                             (pre_q, part, pre_n))
    wait(start(((pre_q, pre_q_h), (part, part_h), (pre_n, pre_n_h), (e1_loc, e1_loc_h), (lat, lat_h), (e_q, e_q_h),
                (oh_q, oh_q_h), (oh_s, oh_s_h), (perm_q, perm_h), (live_q, live_h)), sem_out))


def second_local_kernel(sec, count, src_h, dst_h, lat_h, e_q_h, e_loc_h, oh_q_h, perm_h, ew1, ew2, nw1, nw2,
                        xew1, xew2, xnw1, xnw2, vo_h, vx_h,
                        pre_q_h, part_h, pre_n_h, e1_h_h, out_l_h, n_out, e_out,
                        src, dst, vo, vx, lat, e_q, e_loc, oh_q, perm_q, w, pre_q, part, pre_n, e1_h, own_l, out_l,
                        sem_w, sem_in, sem_out):
    half = src.shape[1] // 2
    mine = sec[0] == 1
    ins = start(((src_h, src), (dst_h, dst), (lat_h, lat), (e_q_h, e_q), (e_loc_h, e_loc), (oh_q_h, oh_q),
                 (perm_h, perm_q), (vo_h, vo), (vx_h, vx)), sem_in)
    weights = fetch_weights(mine, (ew1, ew2, nw1, nw2), (xew1, xew2, xnw1, xnw2), LOCAL, w, sem_w)
    wait(ins)
    eq = e_q[...]
    e1_h[...] = dot_ta(perm_q[...], eq).astype(BF16)
    wait(weights)
    first = e_loc[...]
    second = local_work(count, src, dst, lat[...], eq, first, w, pick_vec(mine, vo, vx), oh_q[...],
                        (pre_q, part, pre_n))

    @pl.when(mine)
    def _():
        own_l[...] = second
        out_l[...] = first

    @pl.when(jnp.logical_not(mine))
    def _():
        own_l[...] = first
        out_l[...] = second

    wait(start(((pre_q, pre_q_h), (part, part_h), (pre_n, pre_n_h), (e1_h, e1_h_h), (out_l, out_l_h),
                (own_l, e_out.at[0, sec[0], pl.ds(half, half)])), sem_out))


def finish(peers, mine, refs, tmp, weights, ins):
    msg, pre_q, vo, vx, live_q, oh_q, part, pre_n, e_q, lat, w = refs
    c_msg, c_pre, c_vo, c_vx, c_live, c_ohq, c_part, c_pren, c_eq, c_lat = ins
    c_msg.wait()
    halo = unpack_rows(msg, tmp, e_q.shape[0], e_q.shape[1], peers)
    wait((c_pre, c_vo, c_vx, weights[0]))
    vec = pick_vec(mine, vo, vx)
    h = pre_q[...] + dot(halo, w[0])
    hid = silu(h).astype(BF16)
    wait((weights[1], c_live, c_ohq, c_part, c_eq))
    y = centre(dot(hid, w[1])) * vec[1:2]
    upd = jnp.where(live_q[:, 0:1] > 0.5, y, 0.0)
    incoming = (part[...] + dot(oh_q[...], upd.astype(BF16))).astype(BF16)
    new_e = (e_q[...].astype(F32) + upd).astype(BF16)
    wait((weights[2], weights[3], c_pren, c_lat))
    hn = silu(pre_n[...] + dot(incoming, w[2])).astype(BF16)
    yn = centre(dot(hn, w[3])) * vec[3:4]
    new_n = (lat[...].astype(F32) + yn).astype(BF16)
    return new_n, new_e


def start_finish(mine, hbm, vmem, own, oth, w, sem_in, sem_w):
    first = start(((hbm[0], vmem[0]),), sem_in)
    weights = fetch_weights(mine, own, oth, FINISH, w, sem_w)
    rest = [pltpu.make_async_copy(a, b, sem_in.at[i + 1]) for i, (a, b) in enumerate(zip(hbm[1:], vmem[1:]))]
    for c in rest:
        c.start()
    return first + rest, weights


def first_finish_kernel(peers, sec, msg_h, pre_q_h, vo_h, vx_h, live_h, oh_q_h, part_h, pre_n_h, e_q_h, lat_h, oh_s_h,
                        ew1, ew2, nw1, nw2, xew1, xew2, xnw1, xnw2, out_msg_h, new_n_h, new_e_h,
                        msg, pre_q, vo, vx, live_q, oh_q, part, pre_n, e_q, lat, oh_s, w, tmp, out_msg, new_n, new_e,
                        sem_w, sem_in, sem_out):
    mine = sec[0] == 0
    hbm = (msg_h, pre_q_h, vo_h, vx_h, live_h, oh_q_h, part_h, pre_n_h, e_q_h, lat_h, oh_s_h)
    vmem = (msg, pre_q, vo, vx, live_q, oh_q, part, pre_n, e_q, lat, oh_s)
    ins, weights = start_finish(mine, hbm, vmem, (ew1, ew2, nw1, nw2), (xew1, xew2, xnw1, xnw2), w, sem_in, sem_w)
    n, e = finish(peers, mine, vmem[:10] + (w,), tmp, weights, ins[:10])
    new_n[...] = n
    new_e[...] = e
    ins[10].wait()
    pack_rows(dot_ta(oh_s[...], n), out_msg, tmp, peers)
    wait(start(((out_msg, out_msg_h), (new_n, new_n_h), (new_e, new_e_h)), sem_out))


def last_finish_kernel(peers, sec, msg_h, pre_q_h, vo_h, vx_h, live_h, oh_q_h, part_h, pre_n_h, e_q_h, lat_h,
                       perm_h, e1_h_h, ew1, ew2, nw1, nw2, xew1, xew2, xnw1, xnw2, n_in, e_in,
                       out_n_h, out_h_h, n_out, e_out,
                       msg, pre_q, vo, vx, live_q, oh_q, part, pre_n, e_q, lat, perm_q, e1_h, w, tmp, new_n, new_h,
                       sem_w, sem_in, sem_out):
    mine = sec[0] == 1
    half = e_q.shape[0]
    hbm = (msg_h, pre_q_h, vo_h, vx_h, live_h, oh_q_h, part_h, pre_n_h, e_q_h, lat_h, perm_h, e1_h_h)
    vmem = (msg, pre_q, vo, vx, live_q, oh_q, part, pre_n, e_q, lat, perm_q, e1_h)
    ins, weights = start_finish(mine, hbm, vmem, (ew1, ew2, nw1, nw2), (xew1, xew2, xnw1, xnw2), w, sem_in, sem_w)
    n, e = finish(peers, mine, vmem[:10] + (w,), tmp, weights, ins[:10])
    new_n[...] = n
    wait(ins[10:])
    new_h[...] = dot_ta(perm_q[...], e).astype(BF16)
    own_n = n_out.at[0, sec[0]]
    own_h = e_out.at[0, sec[0], pl.ds(0, half)]

    @pl.when(mine)
    def _():
        start(((new_n, own_n), (new_h, own_h), (lat, out_n_h), (e1_h, out_h_h)), sem_out)

    @pl.when(jnp.logical_not(mine))
    def _():
        start(((new_n, out_n_h), (new_h, out_h_h), (lat, own_n), (e1_h, own_h)), sem_out)

    wait([pltpu.make_async_copy(a, b, sem_out.at[i]) for i, (a, b) in enumerate(
        ((new_n, out_n_h), (new_h, out_h_h), (lat, own_n), (e1_h, own_h)))])


def other_out_kernel(sec, oth_n, oth_h, oth_l, n_in, e_in, n_out, e_out, sems):
    half = oth_h.shape[0]
    other = 1 - sec[0]
    wait(start((
        (oth_n, n_out.at[0, other]),
        (oth_h, e_out.at[0, other, pl.ds(0, half)]),
        (oth_l, e_out.at[0, other, pl.ds(half, half)]),
    ), sems))


def call(kernel, in_specs, out_specs, out_shapes, scratch, flops, nbytes, limit=LIMIT, **kw):
    return pl.pallas_call(
        kernel,
        out_shape=out_shapes,
        in_specs=in_specs,
        out_specs=out_specs,
        scratch_shapes=scratch,
        compiler_params=pltpu.CompilerParams(vmem_limit_bytes=limit),
        cost_estimate=pl.CostEstimate(flops=flops, bytes_accessed=nbytes, transcendentals=0),
        **kw,
    )


def vmem(x):
    return pltpu.VMEM(x.shape, x.dtype)


def layers(node_feats, edge_feats, edge_src, edge_dst, edge_count, send_rows,
           edge_w1, edge_b1, edge_w2, edge_gain, node_w1, node_b1, node_w2, node_gain):
    _, nodes, width = node_feats.shape
    slots = edge_feats.shape[1]
    half = slots // 2
    peers = send_rows.shape[0]
    sec = lax.axis_index("section").astype(jnp.int32).reshape(1)
    idx = send_rows.T
    src = edge_src.reshape(1, -1)
    dst = edge_dst.reshape(1, -1)
    shape = jax.ShapeDtypeStruct
    nb, nf = shape((nodes, width), BF16), shape((nodes, width), F32)
    hb, hf = shape((half, width), BF16), shape((half, width), F32)
    onehot = shape((nodes, half), BF16)
    live = shape((half, 128), F32)
    msg = shape((half * width // 128, 128), BF16)
    tmp = pltpu.VMEM(msg.shape, F32)
    wts = lambda n: pltpu.VMEM((n, width, width), BF16)
    outs = [shape((1, 2, nodes, width), BF16), shape((1, 2, slots, width), BF16)]

    def DMA(n):
        return pltpu.SemaphoreType.DMA((n,))

    def halo_exchange(m):
        got = lax.all_to_all(m.reshape(peers, -1, 128), "dom", split_axis=0, concat_axis=0, tiled=True)
        return got.reshape(-1, 128)

    def swap(x):
        return lax.ppermute(x, "section", [(0, 1), (1, 0)])

    rows = call(
        functools.partial(select_kernel, peers), [SMEM, ANY, ANY], ANY, msg,
        [vmem(idx), vmem(nb), vmem(msg), tmp, DMA(2)], 10**8, 10**6,
    )(sec, idx, node_feats)
    halo = halo_exchange(rows)
    own_w = (edge_w1, edge_w2, node_w1, node_w2)
    oth_w = []
    for x in own_w:
        oth_w.append(swap(x))
    vec = jnp.concatenate([edge_b1, edge_gain, node_b1, node_gain], axis=0)
    oth_vec = swap(vec)

    res = [hf, nf, nf, hb, nb, hb, onehot, onehot, onehot, live]
    pre_q, part, pre_n, e1_loc, lat, e_q, oh_q, oh_s, perm_q, live_q = call(
        functools.partial(first_local_kernel, peers), [SMEM, SMEM] + [ANY] * 15, [ANY] * 10, res,
        [vmem(x) for x in (src, dst, idx, vec, vec, nb)] + [pltpu.VMEM((slots, width), BF16), wts(5)]
        + [vmem(x) for x in (hf, nf, nf, hb, hb, onehot, onehot, onehot, live)] + [DMA(5), DMA(7), DMA(10)],
        2 * 10**9, 10**7,
    )(sec, edge_count, src, dst, idx, node_feats, edge_feats, *own_w, *oth_w, vec, oth_vec)

    args = (halo, pre_q, vec, oth_vec, live_q, oh_q, part, pre_n, e_q, lat, oh_s)
    rows, n1, e1_q = call(
        functools.partial(first_finish_kernel, peers), [SMEM] + [ANY] * 19, [ANY] * 3, [msg, nb, hb],
        [vmem(x) for x in args] + [wts(4), tmp, vmem(msg), vmem(nb), vmem(hb), DMA(4), DMA(11), DMA(3)],
        10**9, 4 * 10**6,
    )(sec, *args, *own_w, *oth_w)
    halo = halo_exchange(rows)

    args = (n1, e1_q, e1_loc, oh_q, perm_q)
    pre_q, part, pre_n, e1_h, out_l, n_out, e_out = call(
        second_local_kernel, [SMEM, SMEM] + [ANY] * 17, [ANY] * 7, [hf, nf, nf, hb, hb] + outs,
        [vmem(x) for x in (src, dst, vec, vec) + args] + [wts(5)] + [vmem(x) for x in (hf, nf, nf, hb, hb, hb)]
        + [DMA(5), DMA(9), DMA(6)],
        2 * 10**9, 10**7,
    )(sec, edge_count, src, dst, *args, *own_w, *oth_w, vec, oth_vec)
    oth_l = swap(out_l)

    args = (halo, pre_q, vec, oth_vec, live_q, oh_q, part, pre_n, e1_q, n1, perm_q, e1_h)
    out_n, out_h, n_out, e_out = call(
        functools.partial(last_finish_kernel, peers), [SMEM] + [ANY] * 22, [ANY] * 4, [nb, hb] + outs,
        [vmem(x) for x in args] + [wts(4), tmp, vmem(nb), vmem(hb), DMA(4), DMA(12), DMA(4)],
        10**9, 4 * 10**6, input_output_aliases={21: 2, 22: 3},
    )(sec, *args, *own_w, *oth_w, n_out, e_out)
    oth_h = swap(out_h)
    oth_n = swap(out_n)

    return call(other_out_kernel, [SMEM] + [VMEM] * 3 + [ANY, ANY], [ANY, ANY], outs, [DMA(3)], 0, 3 * 10**6,
                limit=1024 * 1024, input_output_aliases={4: 0, 5: 1})(sec, oth_n, oth_h, oth_l, n_out, e_out)


def solution(mesh):
    in_specs = (
        P(None, "dom", None),
        P(None, "dom", None),
        P("dom"),
        P("dom"),
        P("dom"),
        P("dom", None),
        P("section", None, None, None),
        P("section", None),
        P("section", None, None),
        P("section", None),
        P("section", None, None, None),
        P("section", None),
        P("section", None, None),
        P("section", None),
    )
    out_specs = (P("section", None, "dom", None), P("section", None, "dom", None))
    return jax.shard_map(layers, mesh=mesh, in_specs=in_specs, out_specs=out_specs, check_vma=False)
```

```python
import functools

import jax
import jax.numpy as jnp
from jax import lax
from jax.experimental import pallas as pl
from jax.experimental.pallas import tpu as pltpu
from jax.sharding import PartitionSpec as P


F32 = jnp.float32
BF16 = jnp.bfloat16
VMEM = pl.BlockSpec(memory_space=pltpu.VMEM)
SMEM = pl.BlockSpec(memory_space=pltpu.SMEM)
ANY = pl.BlockSpec(memory_space=pl.ANY)
LIMIT = 67043328


def dot(a, b):
    return jnp.dot(a, b, preferred_element_type=F32)


def dot_ta(a, b):
    return lax.dot_general(a, b, (((0,), (0,)), ((), ())), preferred_element_type=F32)


def dot_tb(a, b):
    return lax.dot_general(a, b, (((1,), (1,)), ((), ())), preferred_element_type=F32)


def silu(x):
    half = 0.5 * x
    return half + half * jnp.tanh(half)


def centre(y):
    c = y - jnp.mean(y, axis=-1, keepdims=True)
    var = jnp.mean(c * c, axis=-1, keepdims=True)
    return c * lax.rsqrt(var + 1e-05)


def pick_onehot(row, ids):
    return (ids == row).astype(F32).astype(BF16)


def sublane_ids(rows, cols):
    return lax.broadcasted_iota(jnp.int32, (rows, cols), 0)


def arrival_ids(half, peers, first):
    q = sublane_ids(half, half)
    return first + (half // peers) * (q % peers) + q // peers


def send_onehot(idx, nodes):
    row = jnp.concatenate([idx[k : k + 1] for k in range(idx.shape[0])], axis=1)
    return pick_onehot(row, sublane_ids(nodes, row.shape[1]))


def pack_rows(picked, msg, tmp, peers):
    per, lanes = picked.shape[0] // peers, picked.shape[1] // 128
    for k in range(per):
        for c in range(lanes):
            tmp[pl.ds(k * lanes + c, peers, stride=per * lanes), :] = (
                picked[k * peers : (k + 1) * peers, c * 128 : (c + 1) * 128])
    msg[...] = tmp[...].astype(BF16)


def unpack_rows(msg, tmp, half, width, peers):
    per, lanes = half // peers, width // 128
    tmp[...] = msg[...].astype(F32)
    blocks = [
        jnp.concatenate(
            [tmp[pl.ds(k * lanes + c, peers, stride=per * lanes), :] for c in range(lanes)], axis=1)
        for k in range(per)
    ]
    return jnp.concatenate(blocks, axis=0).astype(BF16)


def start(pairs, sems):
    copies = [pltpu.make_async_copy(a, b, sems.at[i]) for i, (a, b) in enumerate(pairs)]
    for c in copies:
        c.start()
    return copies


def wait(copies):
    for c in copies:
        c.wait()


def matrices(refs):
    ew1, ew2, nw1, nw2 = refs
    return ew1.at[0, 0], ew1.at[0, 1], ew1.at[0, 2], ew2.at[0], nw1.at[0, 0], nw1.at[0, 1], nw2.at[0]


def fetch_weights(mine, own, oth, which, w, sems):
    @pl.when(mine)
    def _():
        start([(matrices(own)[k], w.at[i]) for i, k in enumerate(which)], sems)

    @pl.when(jnp.logical_not(mine))
    def _():
        start([(matrices(oth)[k], w.at[i]) for i, k in enumerate(which)], sems)

    return [pltpu.make_async_copy(matrices(own)[k], w.at[i], sems.at[i]) for i, k in enumerate(which)]


LOCAL = (0, 1, 2, 3, 4)
FINISH = (1, 3, 5, 6)


def select_kernel(peers, sec, idx_h, feats, b0_h, b1_h, b2_h, b3_h, msg_h, vec_h,
                  idx, lat, b0, b1, b2, b3, msg, vec, tmp, sems, sem_out):
    ins = start(((feats.at[sec[0]], lat), (idx_h, idx), (b0_h, b0), (b1_h, b1), (b2_h, b2), (b3_h, b3)), sems)
    wait(ins[1:])
    vec[...] = jnp.concatenate([b[...].astype(F32) for b in (b0, b1, b2, b3)], axis=0).astype(BF16)
    c_vec, = start(((vec, vec_h),), sem_out)
    oh = send_onehot(idx[...], lat.shape[0])
    ins[0].wait()
    pack_rows(dot_ta(oh, lat[...]), msg, tmp, peers)
    wait(start(((msg, msg_h),), sems))
    c_vec.wait()


def local_work(count, src, dst, v, e_halo, e_local, w, vec, oh_q, outs):
    pre_q, part, pre_n = outs
    half = src.shape[1] // 2
    nodes = v.shape[0]
    ids = sublane_ids(nodes, half)
    recv_l = pick_onehot(dst[:, half:], ids)
    send_l = pick_onehot(src[:, half:], ids)
    vs_l = dot_ta(send_l, v).astype(BF16)
    vr_l = dot_ta(recv_l, v).astype(BF16)
    vr_q = dot_ta(oh_q, v).astype(BF16)
    pre_q[...] = dot(e_halo, w[0]) + dot(vr_q, w[2]) + vec[0:1]
    h = dot(e_local, w[0]) + dot(vs_l, w[1]) + dot(vr_l, w[2]) + vec[0:1]
    y = centre(dot(silu(h).astype(BF16), w[3])) * vec[1:2]
    pos = sublane_ids(half, 1) + half
    upd = jnp.where(pos < count[0], y, 0.0)
    part[...] = dot(recv_l, upd.astype(BF16))
    pre_n[...] = dot(v, w[4]) + vec[2:3]
    return (e_local.astype(F32) + upd).astype(BF16)


def pick_vec(mine, vec_own, vec_oth):
    return jnp.where(mine, vec_own[...].astype(F32), vec_oth[...].astype(F32))


def first_local_kernel(peers, sec, count, src_h, dst_h, idx_h, nfeats, efeats, ew1, ew2, nw1, nw2,
                       xew1, xew2, xnw1, xnw2, vo_h, vx_h,
                       pre_q_h, part_h, pre_n_h, e1_loc_h, lat_h, e_q_h, oh_q_h, oh_s_h, perm_h, live_h,
                       src, dst, idx, vo, vx, lat, e, w, pre_q, part, pre_n, e1_loc, e_q, oh_q, oh_s, perm_q, live_q,
                       sem_w, sem_in, sem_out):
    half = src.shape[1] // 2
    nodes = lat.shape[0]
    mine = sec[0] == 0
    ins = start(((src_h, src), (dst_h, dst), (idx_h, idx), (efeats.at[sec[0]], e), (nfeats.at[sec[0]], lat),
                 (vo_h, vo), (vx_h, vx)), sem_in)
    weights = fetch_weights(mine, (ew1, ew2, nw1, nw2), (xew1, xew2, xnw1, xnw2), LOCAL, w, sem_w)
    wait(ins)
    oh_s[...] = send_onehot(idx[...], nodes)
    perm = pick_onehot(src[:, :half], arrival_ids(half, peers, nodes))
    perm_q[...] = perm
    recv_h = pick_onehot(dst[:, :half], sublane_ids(nodes, half))
    ohq = dot_tb(recv_h, perm).astype(BF16)
    oh_q[...] = ohq
    pos = lax.broadcasted_iota(jnp.int32, (half, half), 1)
    live = jnp.sum(jnp.where(pos < count[0], perm.astype(F32), 0.0), axis=1, keepdims=True)
    live_q[...] = jnp.broadcast_to(live, live_q.shape)
    eq = dot(perm, e[:half]).astype(BF16)
    e_q[...] = eq
    wait(weights)
    e1_loc[...] = local_work(count, src, dst, lat[...], eq, e[half:], w, pick_vec(mine, vo, vx), ohq,
                             (pre_q, part, pre_n))
    wait(start(((pre_q, pre_q_h), (part, part_h), (pre_n, pre_n_h), (e1_loc, e1_loc_h), (lat, lat_h), (e_q, e_q_h),
                (oh_q, oh_q_h), (oh_s, oh_s_h), (perm_q, perm_h), (live_q, live_h)), sem_out))


def second_local_kernel(sec, count, src_h, dst_h, lat_h, e_q_h, e_loc_h, oh_q_h, perm_h, ew1, ew2, nw1, nw2,
                        xew1, xew2, xnw1, xnw2, vo_h, vx_h,
                        pre_q_h, part_h, pre_n_h, e1_h_h, out_l_h, n_out, e_out,
                        src, dst, vo, vx, lat, e_q, e_loc, oh_q, perm_q, w, pre_q, part, pre_n, e1_h, own_l, out_l,
                        sem_w, sem_in, sem_out):
    half = src.shape[1] // 2
    mine = sec[0] == 1
    ins = start(((src_h, src), (dst_h, dst), (lat_h, lat), (e_q_h, e_q), (e_loc_h, e_loc), (oh_q_h, oh_q),
                 (perm_h, perm_q), (vo_h, vo), (vx_h, vx)), sem_in)
    weights = fetch_weights(mine, (ew1, ew2, nw1, nw2), (xew1, xew2, xnw1, xnw2), LOCAL, w, sem_w)
    wait(ins)
    eq = e_q[...]
    e1_h[...] = dot_ta(perm_q[...], eq).astype(BF16)
    wait(weights)
    first = e_loc[...]
    second = local_work(count, src, dst, lat[...], eq, first, w, pick_vec(mine, vo, vx), oh_q[...],
                        (pre_q, part, pre_n))

    @pl.when(mine)
    def _():
        own_l[...] = second
        out_l[...] = first

    @pl.when(jnp.logical_not(mine))
    def _():
        own_l[...] = first
        out_l[...] = second

    wait(start(((pre_q, pre_q_h), (part, part_h), (pre_n, pre_n_h), (e1_h, e1_h_h), (out_l, out_l_h),
                (own_l, e_out.at[0, sec[0], pl.ds(half, half)])), sem_out))


def finish(peers, mine, refs, tmp, weights, ins):
    msg, pre_q, vo, vx, live_q, oh_q, part, pre_n, e_q, lat, w = refs
    c_msg, c_pre, c_vo, c_vx, c_live, c_ohq, c_part, c_pren, c_eq, c_lat = ins
    c_msg.wait()
    halo = unpack_rows(msg, tmp, e_q.shape[0], e_q.shape[1], peers)
    wait((c_pre, c_vo, c_vx, weights[0]))
    vec = pick_vec(mine, vo, vx)
    h = pre_q[...] + dot(halo, w[0])
    hid = silu(h).astype(BF16)
    wait((weights[1], c_live, c_ohq, c_part, c_eq))
    y = centre(dot(hid, w[1])) * vec[1:2]
    upd = jnp.where(live_q[:, 0:1] > 0.5, y, 0.0)
    incoming = (part[...] + dot(oh_q[...], upd.astype(BF16))).astype(BF16)
    new_e = (e_q[...].astype(F32) + upd).astype(BF16)
    wait((weights[2], weights[3], c_pren, c_lat))
    hn = silu(pre_n[...] + dot(incoming, w[2])).astype(BF16)
    yn = centre(dot(hn, w[3])) * vec[3:4]
    new_n = (lat[...].astype(F32) + yn).astype(BF16)
    return new_n, new_e


def start_finish(mine, hbm, vmem, own, oth, w, sem_in, sem_w):
    first = start(((hbm[0], vmem[0]),), sem_in)
    weights = fetch_weights(mine, own, oth, FINISH, w, sem_w)
    rest = [pltpu.make_async_copy(a, b, sem_in.at[i + 1]) for i, (a, b) in enumerate(zip(hbm[1:], vmem[1:]))]
    for c in rest:
        c.start()
    return first + rest, weights


def first_finish_kernel(peers, sec, msg_h, pre_q_h, vo_h, vx_h, live_h, oh_q_h, part_h, pre_n_h, e_q_h, lat_h, oh_s_h,
                        ew1, ew2, nw1, nw2, xew1, xew2, xnw1, xnw2, out_msg_h, new_n_h, new_e_h,
                        msg, pre_q, vo, vx, live_q, oh_q, part, pre_n, e_q, lat, oh_s, w, tmp, out_msg, new_n, new_e,
                        sem_w, sem_in, sem_out):
    mine = sec[0] == 0
    hbm = (msg_h, pre_q_h, vo_h, vx_h, live_h, oh_q_h, part_h, pre_n_h, e_q_h, lat_h, oh_s_h)
    vmem = (msg, pre_q, vo, vx, live_q, oh_q, part, pre_n, e_q, lat, oh_s)
    ins, weights = start_finish(mine, hbm, vmem, (ew1, ew2, nw1, nw2), (xew1, xew2, xnw1, xnw2), w, sem_in, sem_w)
    n, e = finish(peers, mine, vmem[:10] + (w,), tmp, weights, ins[:10])
    new_n[...] = n
    new_e[...] = e
    ins[10].wait()
    pack_rows(dot_ta(oh_s[...], n), out_msg, tmp, peers)
    wait(start(((out_msg, out_msg_h), (new_n, new_n_h), (new_e, new_e_h)), sem_out))


def last_finish_kernel(peers, sec, msg_h, pre_q_h, vo_h, vx_h, live_h, oh_q_h, part_h, pre_n_h, e_q_h, lat_h,
                       perm_h, e1_h_h, oth_l_h, ew1, ew2, nw1, nw2, xew1, xew2, xnw1, xnw2, n_in, e_in,
                       out_n_h, out_h_h, n_out, e_out,
                       msg, pre_q, vo, vx, live_q, oh_q, part, pre_n, e_q, lat, perm_q, e1_h, oth_l,
                       w, tmp, new_n, new_h, sem_w, sem_in, sem_out):
    mine = sec[0] == 1
    half = e_q.shape[0]
    hbm = (msg_h, pre_q_h, vo_h, vx_h, live_h, oh_q_h, part_h, pre_n_h, e_q_h, lat_h, perm_h, e1_h_h, oth_l_h)
    vmem = (msg, pre_q, vo, vx, live_q, oh_q, part, pre_n, e_q, lat, perm_q, e1_h, oth_l)
    ins, weights = start_finish(mine, hbm, vmem, (ew1, ew2, nw1, nw2), (xew1, xew2, xnw1, xnw2), w, sem_in, sem_w)
    n, e = finish(peers, mine, vmem[:10] + (w,), tmp, weights, ins[:10])
    new_n[...] = n
    wait(ins[10:])
    c_oth = pltpu.make_async_copy(oth_l, e_out.at[0, 1 - sec[0], pl.ds(half, half)], sem_out.at[4])
    c_oth.start()
    new_h[...] = dot_ta(perm_q[...], e).astype(BF16)
    own_n = n_out.at[0, sec[0]]
    own_h = e_out.at[0, sec[0], pl.ds(0, half)]

    @pl.when(mine)
    def _():
        start(((new_n, own_n), (new_h, own_h), (lat, out_n_h), (e1_h, out_h_h)), sem_out)

    @pl.when(jnp.logical_not(mine))
    def _():
        start(((new_n, out_n_h), (new_h, out_h_h), (lat, own_n), (e1_h, own_h)), sem_out)

    wait([pltpu.make_async_copy(a, b, sem_out.at[i]) for i, (a, b) in enumerate(
        ((new_n, out_n_h), (new_h, out_h_h), (lat, own_n), (e1_h, own_h)))])
    c_oth.wait()


def other_out_kernel(sec, oth_n, oth_h, n_in, e_in, n_out, e_out, sems):
    half = oth_h.shape[0]
    other = 1 - sec[0]
    wait(start((
        (oth_n, n_out.at[0, other]),
        (oth_h, e_out.at[0, other, pl.ds(0, half)]),
    ), sems))


def call(kernel, in_specs, out_specs, out_shapes, scratch, flops, nbytes, limit=LIMIT - 65536, **kw):
    return pl.pallas_call(
        kernel,
        out_shape=out_shapes,
        in_specs=in_specs,
        out_specs=out_specs,
        scratch_shapes=scratch,
        compiler_params=pltpu.CompilerParams(vmem_limit_bytes=limit),
        cost_estimate=pl.CostEstimate(flops=flops, bytes_accessed=nbytes, transcendentals=0),
        **kw,
    )


def vmem(x):
    return pltpu.VMEM(x.shape, x.dtype)


def layers(node_feats, edge_feats, edge_src, edge_dst, edge_count, send_rows,
           edge_w1, edge_b1, edge_w2, edge_gain, node_w1, node_b1, node_w2, node_gain):
    _, nodes, width = node_feats.shape
    slots = edge_feats.shape[1]
    half = slots // 2
    peers = send_rows.shape[0]
    sec = lax.axis_index("section").astype(jnp.int32).reshape(1)
    idx = send_rows.T
    src = edge_src.reshape(1, -1)
    dst = edge_dst.reshape(1, -1)
    shape = jax.ShapeDtypeStruct
    nb, nf = shape((nodes, width), BF16), shape((nodes, width), F32)
    hb, hf = shape((half, width), BF16), shape((half, width), F32)
    onehot = shape((nodes, half), BF16)
    live = shape((half, 128), F32)
    msg = shape((half * width // 128, 128), BF16)
    tmp = pltpu.VMEM(msg.shape, F32)
    wts = lambda n: pltpu.VMEM((n, width, width), BF16)
    outs = [shape((1, 2, nodes, width), BF16), shape((1, 2, slots, width), BF16)]

    def DMA(n):
        return pltpu.SemaphoreType.DMA((n,))

    def halo_exchange(m):
        got = lax.all_to_all(m.reshape(peers, -1, 128), "dom", split_axis=0, concat_axis=0, tiled=True)
        return got.reshape(-1, 128)

    def swap(x):
        return lax.ppermute(x, "section", [(0, 1), (1, 0)])

    rows, vec = call(
        functools.partial(select_kernel, peers), [SMEM] + [ANY] * 6, [ANY, ANY], [msg, shape((4, width), BF16)],
        [vmem(idx), vmem(nb)] + [vmem(edge_b1)] * 4 + [vmem(msg), pltpu.VMEM((4, width), BF16), tmp, DMA(6), DMA(1)],
        10**8, 10**6, limit=LIMIT,
    )(sec, idx, node_feats, edge_b1, edge_gain, node_b1, node_gain)
    halo = halo_exchange(rows)
    own_w = (edge_w1, edge_w2, node_w1, node_w2)
    oth_w = []
    for x in own_w:
        oth_w.append(swap(x))
    oth_vec = swap(vec)

    res = [hf, nf, nf, hb, nb, hb, onehot, onehot, onehot, live]
    pre_q, part, pre_n, e1_loc, lat, e_q, oh_q, oh_s, perm_q, live_q = call(
        functools.partial(first_local_kernel, peers), [SMEM, SMEM] + [ANY] * 15, [ANY] * 10, res,
        [vmem(x) for x in (src, dst, idx, vec, vec, nb)] + [pltpu.VMEM((slots, width), BF16), wts(5)]
        + [vmem(x) for x in (hf, nf, nf, hb, hb, onehot, onehot, onehot, live)] + [DMA(5), DMA(7), DMA(10)],
        2 * 10**9, 10**7,
    )(sec, edge_count, src, dst, idx, node_feats, edge_feats, *own_w, *oth_w, vec, oth_vec)

    args = (halo, pre_q, vec, oth_vec, live_q, oh_q, part, pre_n, e_q, lat, oh_s)
    rows, n1, e1_q = call(
        functools.partial(first_finish_kernel, peers), [SMEM] + [ANY] * 19, [ANY] * 3, [msg, nb, hb],
        [vmem(x) for x in args] + [wts(4), tmp, vmem(msg), vmem(nb), vmem(hb), DMA(4), DMA(11), DMA(3)],
        10**9, 4 * 10**6,
    )(sec, *args, *own_w, *oth_w)
    halo = halo_exchange(rows)

    args = (n1, e1_q, e1_loc, oh_q, perm_q)
    pre_q, part, pre_n, e1_h, out_l, n_out, e_out = call(
        second_local_kernel, [SMEM, SMEM] + [ANY] * 17, [ANY] * 7, [hf, nf, nf, hb, hb] + outs,
        [vmem(x) for x in (src, dst, vec, vec) + args] + [wts(5)] + [vmem(x) for x in (hf, nf, nf, hb, hb, hb)]
        + [DMA(5), DMA(9), DMA(6)],
        2 * 10**9, 10**7,
    )(sec, edge_count, src, dst, *args, *own_w, *oth_w, vec, oth_vec)
    oth_l = swap(out_l)

    args = (halo, pre_q, vec, oth_vec, live_q, oh_q, part, pre_n, e1_q, n1, perm_q, e1_h, oth_l)
    out_n, out_h, n_out, e_out = call(
        functools.partial(last_finish_kernel, peers), [SMEM] + [ANY] * 23, [ANY] * 4, [nb, hb] + outs,
        [vmem(x) for x in args] + [wts(4), tmp, vmem(nb), vmem(hb), DMA(4), DMA(13), DMA(5)],
        10**9, 4 * 10**6, input_output_aliases={22: 2, 23: 3},
    )(sec, *args, *own_w, *oth_w, n_out, e_out)
    oth_h = swap(out_h)
    oth_n = swap(out_n)

    return call(other_out_kernel, [SMEM] + [VMEM] * 2 + [ANY, ANY], [ANY, ANY], outs, [DMA(2)], 0, 3 * 10**6,
                limit=1024 * 1024, input_output_aliases={3: 0, 4: 1})(sec, oth_n, oth_h, n_out, e_out)


def solution(mesh):
    in_specs = (
        P(None, "dom", None),
        P(None, "dom", None),
        P("dom"),
        P("dom"),
        P("dom"),
        P("dom", None),
        P("section", None, None, None),
        P("section", None),
        P("section", None, None),
        P("section", None),
        P("section", None, None, None),
        P("section", None),
        P("section", None, None),
        P("section", None),
    )
    out_specs = (P("section", None, "dom", None), P("section", None, "dom", None))
    return jax.shard_map(layers, mesh=mesh, in_specs=in_specs, out_specs=out_specs, check_vma=False)
```

```python
import functools

import jax
import jax.numpy as jnp
from jax import lax
from jax.experimental import pallas as pl
from jax.experimental.pallas import tpu as pltpu
from jax.sharding import PartitionSpec as P


F32 = jnp.float32
BF16 = jnp.bfloat16
VMEM = pl.BlockSpec(memory_space=pltpu.VMEM)
SMEM = pl.BlockSpec(memory_space=pltpu.SMEM)
ANY = pl.BlockSpec(memory_space=pl.ANY)
LIMIT = 67043328


def dot(a, b):
    return jnp.dot(a, b, preferred_element_type=F32)


def dot_ta(a, b):
    return lax.dot_general(a, b, (((0,), (0,)), ((), ())), preferred_element_type=F32)


def dot_tb(a, b):
    return lax.dot_general(a, b, (((1,), (1,)), ((), ())), preferred_element_type=F32)


def silu(x):
    half = 0.5 * x
    return half + half * jnp.tanh(half)


def centre(y):
    c = y - jnp.mean(y, axis=-1, keepdims=True)
    var = jnp.mean(c * c, axis=-1, keepdims=True)
    return c * lax.rsqrt(var + 1e-05)


def pick_onehot(row, ids):
    return (ids == row).astype(F32).astype(BF16)


def sublane_ids(rows, cols):
    return lax.broadcasted_iota(jnp.int32, (rows, cols), 0)


def arrival_ids(half, peers, first):
    q = sublane_ids(half, half)
    return first + (half // peers) * (q % peers) + q // peers


def send_onehot(idx, nodes):
    row = jnp.concatenate([idx[k : k + 1] for k in range(idx.shape[0])], axis=1)
    return pick_onehot(row, sublane_ids(nodes, row.shape[1]))


def pack_rows(picked, msg, tmp, peers):
    per, lanes = picked.shape[0] // peers, picked.shape[1] // 128
    for k in range(per):
        for c in range(lanes):
            tmp[pl.ds(k * lanes + c, peers, stride=per * lanes), :] = (
                picked[k * peers : (k + 1) * peers, c * 128 : (c + 1) * 128])
    msg[...] = tmp[...].astype(BF16)


def unpack_rows(msg, tmp, half, width, peers):
    per, lanes = half // peers, width // 128
    tmp[...] = msg[...].astype(F32)
    blocks = [
        jnp.concatenate(
            [tmp[pl.ds(k * lanes + c, peers, stride=per * lanes), :] for c in range(lanes)], axis=1)
        for k in range(per)
    ]
    return jnp.concatenate(blocks, axis=0).astype(BF16)


def start(pairs, sems):
    copies = [pltpu.make_async_copy(a, b, sems.at[i]) for i, (a, b) in enumerate(pairs)]
    for c in copies:
        c.start()
    return copies


def wait(copies):
    for c in copies:
        c.wait()


def matrices(refs):
    ew1, ew2, nw1 = refs[:3]
    return (ew1.at[0, 0], ew1.at[0, 1], ew1.at[0, 2], ew2.at[0], nw1.at[0, 0], nw1.at[0, 1]) + tuple(
        r.at[0] for r in refs[3:])


def fetch_weights(mine, own, oth, which, w, sems):
    @pl.when(mine)
    def _():
        start([(matrices(own)[k], w.at[i]) for i, k in enumerate(which)], sems)

    @pl.when(jnp.logical_not(mine))
    def _():
        start([(matrices(oth)[k], w.at[i]) for i, k in enumerate(which)], sems)

    return [pltpu.make_async_copy(matrices(own)[k], w.at[i], sems.at[i]) for i, k in enumerate(which)]


LOCAL = (0, 1, 2, 3, 4)
FINISH = (1, 3, 5, 6)


def select_kernel(peers, sec, idx_h, feats, b0_h, b1_h, b2_h, b3_h, msg_h, vec_h,
                  idx, lat, b0, b1, b2, b3, msg, vec, tmp, sems, sem_out):
    ins = start(((feats.at[sec[0]], lat), (idx_h, idx), (b0_h, b0), (b1_h, b1), (b2_h, b2), (b3_h, b3)), sems)
    wait(ins[1:])
    vec[...] = jnp.concatenate([b[...].astype(F32) for b in (b0, b1, b2, b3)], axis=0).astype(BF16)
    c_vec, = start(((vec, vec_h),), sem_out)
    oh = send_onehot(idx[...], lat.shape[0])
    ins[0].wait()
    pack_rows(dot_ta(oh, lat[...]), msg, tmp, peers)
    wait(start(((msg, msg_h),), sems))
    c_vec.wait()


def local_work(count, src, dst, v, e_halo, e_local, w, vec, oh_q, outs):
    pre_q, part, pre_n = outs
    half = src.shape[1] // 2
    nodes = v.shape[0]
    ids = sublane_ids(nodes, half)
    recv_l = pick_onehot(dst[:, half:], ids)
    send_l = pick_onehot(src[:, half:], ids)
    vs_l = dot_ta(send_l, v).astype(BF16)
    vr_l = dot_ta(recv_l, v).astype(BF16)
    vr_q = dot_ta(oh_q, v).astype(BF16)
    pre_q[...] = dot(e_halo, w[0]) + dot(vr_q, w[2]) + vec[0:1]
    h = dot(e_local, w[0]) + dot(vs_l, w[1]) + dot(vr_l, w[2]) + vec[0:1]
    y = centre(dot(silu(h).astype(BF16), w[3])) * vec[1:2]
    pos = sublane_ids(half, 1) + half
    upd = jnp.where(pos < count[0], y, 0.0)
    part[...] = dot(recv_l, upd.astype(BF16))
    pre_n[...] = dot(v, w[4]) + vec[2:3]
    return (e_local.astype(F32) + upd).astype(BF16)


def pick_vec(mine, vec_own, vec_oth):
    return jnp.where(mine, vec_own[...].astype(F32), vec_oth[...].astype(F32))


def first_local_kernel(peers, sec, count, src_h, dst_h, idx_h, nfeats, efeats, ew1, ew2, nw1,
                       xew1, xew2, xnw1, vo_h, vx_h,
                       pre_q_h, part_h, pre_n_h, e1_loc_h, lat_h, e_q_h, oh_q_h, oh_s_h, perm_h, live_h,
                       src, dst, idx, vo, vx, lat, e, w, pre_q, part, pre_n, e1_loc, e_q, oh_q, oh_s, perm_q, live_q,
                       sem_w, sem_in, sem_out):
    half = src.shape[1] // 2
    nodes = lat.shape[0]
    mine = sec[0] == 0
    ins = start(((src_h, src), (dst_h, dst), (idx_h, idx), (efeats.at[sec[0]], e), (nfeats.at[sec[0]], lat),
                 (vo_h, vo), (vx_h, vx)), sem_in)
    weights = fetch_weights(mine, (ew1, ew2, nw1), (xew1, xew2, xnw1), LOCAL, w, sem_w)
    wait(ins)
    oh_s[...] = send_onehot(idx[...], nodes)
    perm = pick_onehot(src[:, :half], arrival_ids(half, peers, nodes))
    perm_q[...] = perm
    recv_h = pick_onehot(dst[:, :half], sublane_ids(nodes, half))
    ohq = dot_tb(recv_h, perm).astype(BF16)
    oh_q[...] = ohq
    pos = lax.broadcasted_iota(jnp.int32, (half, half), 1)
    live = jnp.sum(jnp.where(pos < count[0], perm.astype(F32), 0.0), axis=1, keepdims=True)
    live_q[...] = jnp.broadcast_to(live, live_q.shape)
    eq = dot(perm, e[:half]).astype(BF16)
    e_q[...] = eq
    wait(weights)
    e1_loc[...] = local_work(count, src, dst, lat[...], eq, e[half:], w, pick_vec(mine, vo, vx), ohq,
                             (pre_q, part, pre_n))
    wait(start(((pre_q, pre_q_h), (part, part_h), (pre_n, pre_n_h), (e1_loc, e1_loc_h), (lat, lat_h), (e_q, e_q_h),
                (oh_q, oh_q_h), (oh_s, oh_s_h), (perm_q, perm_h), (live_q, live_h)), sem_out))


def second_local_kernel(sec, count, src_h, dst_h, lat_h, e_q_h, e_loc_h, oh_q_h, perm_h, ew1, ew2, nw1,
                        xew1, xew2, xnw1, vo_h, vx_h,
                        pre_q_h, part_h, pre_n_h, e1_h_h, out_l_h, e_out,
                        src, dst, vo, vx, lat, e_q, e_loc, oh_q, perm_q, w, pre_q, part, pre_n, e1_h, own_l, out_l,
                        sem_w, sem_in, sem_out):
    half = src.shape[1] // 2
    mine = sec[0] == 1
    ins = start(((src_h, src), (dst_h, dst), (lat_h, lat), (e_q_h, e_q), (e_loc_h, e_loc), (oh_q_h, oh_q),
                 (perm_h, perm_q), (vo_h, vo), (vx_h, vx)), sem_in)
    weights = fetch_weights(mine, (ew1, ew2, nw1), (xew1, xew2, xnw1), LOCAL, w, sem_w)
    wait(ins)
    eq = e_q[...]
    e1_h[...] = dot_ta(perm_q[...], eq).astype(BF16)
    wait(weights)
    first = e_loc[...]
    second = local_work(count, src, dst, lat[...], eq, first, w, pick_vec(mine, vo, vx), oh_q[...],
                        (pre_q, part, pre_n))

    @pl.when(mine)
    def _():
        own_l[...] = second
        out_l[...] = first

    @pl.when(jnp.logical_not(mine))
    def _():
        own_l[...] = first
        out_l[...] = second

    wait(start(((pre_q, pre_q_h), (part, part_h), (pre_n, pre_n_h), (e1_h, e1_h_h), (out_l, out_l_h),
                (own_l, e_out.at[0, sec[0], pl.ds(half, half)])), sem_out))


def finish(peers, mine, refs, waits, on_edges):
    msg, pre_q, vo, vx, live_q, oh_q, part, e_q, pre_n, lat, w, tmp = refs
    waits[0]()
    halo = unpack_rows(msg, tmp, e_q.shape[0], e_q.shape[1], peers)
    waits[1]()
    vec = pick_vec(mine, vo, vx)
    h = pre_q[...] + dot(halo, w[0])
    hid = silu(h).astype(BF16)
    waits[2]()
    y = centre(dot(hid, w[1])) * vec[1:2]
    upd = jnp.where(live_q[:, 0:1] > 0.5, y, 0.0)
    incoming = (part[...] + dot(oh_q[...], upd.astype(BF16))).astype(BF16)
    on_edges((e_q[...].astype(F32) + upd).astype(BF16))
    hn = silu(pre_n[...] + dot(incoming, w[2])).astype(BF16)
    yn = centre(dot(hn, w[3])) * vec[3:4]
    return (lat[...].astype(F32) + yn).astype(BF16)


def start_finish(mine, hbm, vmem, own, oth, w, sem_in, sem_w):
    def copies(refs):
        m = [matrices(refs)[k] for k in FINISH]
        data = [pltpu.make_async_copy(a, b, sem_in.at[i]) for i, (a, b) in enumerate(zip(hbm, vmem))]
        mats = [pltpu.make_async_copy(a, w.at[i], sem_w.at[i]) for i, a in enumerate(m)]
        return data[:1], [mats[0]] + data[1:4], [mats[1]] + data[4:8] + mats[2:] + data[8:]

    def go(refs):
        for group in copies(refs):
            for c in group:
                c.start()

    @pl.when(mine)
    def _():
        go(own)

    @pl.when(jnp.logical_not(mine))
    def _():
        go(oth)

    return [functools.partial(wait, group) for group in copies(own)]


def first_finish_kernel(peers, sec, msg_h, pre_q_h, vo_h, vx_h, live_h, oh_q_h, part_h, e_q_h, pre_n_h, lat_h, oh_s_h,
                        ew1, ew2, nw1, nw2, xew1, xew2, xnw1, xnw2, out_msg_h, new_n_h, new_e_h,
                        msg, pre_q, vo, vx, live_q, oh_q, part, e_q, pre_n, lat, oh_s, w, tmp, out_msg, new_n, new_e,
                        sem_w, sem_in, sem_out):
    mine = sec[0] == 0
    hbm = (msg_h, pre_q_h, vo_h, vx_h, live_h, oh_q_h, part_h, e_q_h, pre_n_h, lat_h, oh_s_h)
    vmem = (msg, pre_q, vo, vx, live_q, oh_q, part, e_q, pre_n, lat, oh_s)
    waits = start_finish(mine, hbm, vmem, (ew1, ew2, nw1, nw2), (xew1, xew2, xnw1, xnw2), w, sem_in, sem_w)
    c_msg, c_n, c_e = [pltpu.make_async_copy(a, b, sem_out.at[i]) for i, (a, b) in enumerate(
        ((out_msg, out_msg_h), (new_n, new_n_h), (new_e, new_e_h)))]

    def on_edges(e):
        new_e[...] = e
        c_e.start()

    n = finish(peers, mine, vmem[:10] + (w, tmp), waits, on_edges)
    new_n[...] = n
    pack_rows(dot_ta(oh_s[...], n), out_msg, tmp, peers)
    c_msg.start()
    c_n.start()
    wait((c_e, c_msg, c_n))


def last_finish_kernel(peers, sec, msg_h, pre_q_h, vo_h, vx_h, live_h, oh_q_h, part_h, e_q_h, pre_n_h, lat_h,
                       perm_h, e1_h_h, oth_l_h, ew1, ew2, nw1, nw2, xew1, xew2, xnw1, xnw2, e_in,
                       cross, n_out, e_out,
                       msg, pre_q, vo, vx, live_q, oh_q, part, e_q, pre_n, lat, perm_q, e1_h, oth_l,
                       w, tmp, own_h, out_h, own_n, out_n, sem_w, sem_in, sem_out):
    mine = sec[0] == 1
    half, nodes = e_q.shape[0], lat.shape[0]
    hbm = (msg_h, pre_q_h, vo_h, vx_h, live_h, oh_q_h, part_h, e_q_h, pre_n_h, lat_h, perm_h, e1_h_h, oth_l_h)
    vmem = (msg, pre_q, vo, vx, live_q, oh_q, part, e_q, pre_n, lat, perm_q, e1_h, oth_l)
    waits = start_finish(mine, hbm, vmem, (ew1, ew2, nw1, nw2), (xew1, xew2, xnw1, xnw2), w, sem_in, sem_w)
    writes = [pltpu.make_async_copy(a, b, sem_out.at[i]) for i, (a, b) in enumerate((
        (out_h, cross.at[pl.ds(nodes, half)]),
        (own_h, e_out.at[0, sec[0], pl.ds(0, half)]),
        (oth_l, e_out.at[0, 1 - sec[0], pl.ds(half, half)]),
        (out_n, cross.at[pl.ds(0, nodes)]),
        (own_n, n_out.at[0, sec[0]]),
    ))]

    def on_edges(e):
        new_h = dot_ta(perm_q[...], e)
        old_h = e1_h[...].astype(F32)
        out_h[...] = jnp.where(mine, old_h, new_h).astype(BF16)
        own_h[...] = jnp.where(mine, new_h, old_h).astype(BF16)
        for c in writes[:3]:
            c.start()

    n = finish(peers, mine, vmem[:10] + (w, tmp), waits, on_edges).astype(F32)
    old_n = lat[...].astype(F32)
    out_n[...] = jnp.where(mine, old_n, n).astype(BF16)
    own_n[...] = jnp.where(mine, n, old_n).astype(BF16)
    for c in writes[3:]:
        c.start()
    wait(writes)


def other_out_kernel(sec, crossed, n_in, e_in, n_out, e_out, sems):
    nodes, slots = n_out.shape[2], e_out.shape[2]
    other = 1 - sec[0]
    wait(start((
        (crossed.at[pl.ds(0, nodes)], n_out.at[0, other]),
        (crossed.at[pl.ds(nodes, slots // 2)], e_out.at[0, other, pl.ds(0, slots // 2)]),
    ), sems))


def call(kernel, in_specs, out_specs, out_shapes, scratch, flops, nbytes, limit=LIMIT - 65536, **kw):
    return pl.pallas_call(
        kernel,
        out_shape=out_shapes,
        in_specs=in_specs,
        out_specs=out_specs,
        scratch_shapes=scratch,
        compiler_params=pltpu.CompilerParams(vmem_limit_bytes=limit),
        cost_estimate=pl.CostEstimate(flops=flops, bytes_accessed=nbytes, transcendentals=0),
        **kw,
    )


def vmem(x):
    return pltpu.VMEM(x.shape, x.dtype)


def layers(node_feats, edge_feats, edge_src, edge_dst, edge_count, send_rows,
           edge_w1, edge_b1, edge_w2, edge_gain, node_w1, node_b1, node_w2, node_gain):
    _, nodes, width = node_feats.shape
    slots = edge_feats.shape[1]
    half = slots // 2
    peers = send_rows.shape[0]
    sec = lax.axis_index("section").astype(jnp.int32).reshape(1)
    idx = send_rows.T
    src = edge_src.reshape(1, -1)
    dst = edge_dst.reshape(1, -1)
    shape = jax.ShapeDtypeStruct
    nb, nf = shape((nodes, width), BF16), shape((nodes, width), F32)
    hb, hf = shape((half, width), BF16), shape((half, width), F32)
    onehot = shape((nodes, half), BF16)
    live = shape((half, 128), F32)
    msg = shape((half * width // 128, 128), BF16)
    tmp = pltpu.VMEM(msg.shape, F32)
    wts = lambda n: pltpu.VMEM((n, width, width), BF16)
    outs = [shape((1, 2, nodes, width), BF16), shape((1, 2, slots, width), BF16)]

    def DMA(n):
        return pltpu.SemaphoreType.DMA((n,))

    def halo_exchange(m):
        got = lax.all_to_all(m.reshape(peers, -1, 128), "dom", split_axis=0, concat_axis=0, tiled=True)
        return got.reshape(-1, 128)

    def swap(x):
        return lax.ppermute(x, "section", [(0, 1), (1, 0)])

    rows, vec = call(
        functools.partial(select_kernel, peers), [SMEM] + [ANY] * 6, [ANY, ANY], [msg, shape((4, width), BF16)],
        [vmem(idx), vmem(nb)] + [vmem(edge_b1)] * 4 + [vmem(msg), pltpu.VMEM((4, width), BF16), tmp, DMA(6), DMA(1)],
        10**8, 10**6, limit=LIMIT,
    )(sec, idx, node_feats, edge_b1, edge_gain, node_b1, node_gain)
    halo = halo_exchange(rows)
    own_w = (edge_w1, edge_w2, node_w1, node_w2)
    oth_w = []
    for x in own_w:
        oth_w.append(swap(x))
    oth_vec = swap(vec)

    res = [hf, nf, nf, hb, nb, hb, onehot, onehot, onehot, live]
    pre_q, part, pre_n, e1_loc, lat, e_q, oh_q, oh_s, perm_q, live_q = call(
        functools.partial(first_local_kernel, peers), [SMEM, SMEM] + [ANY] * 13, [ANY] * 10, res,
        [vmem(x) for x in (src, dst, idx, vec, vec, nb)] + [pltpu.VMEM((slots, width), BF16), wts(5)]
        + [vmem(x) for x in (hf, nf, nf, hb, hb, onehot, onehot, onehot, live)] + [DMA(5), DMA(7), DMA(10)],
        2 * 10**9, 10**7,
    )(sec, edge_count, src, dst, idx, node_feats, edge_feats, *own_w[:3], *oth_w[:3], vec, oth_vec)

    args = (halo, pre_q, vec, oth_vec, live_q, oh_q, part, e_q, pre_n, lat, oh_s)
    rows, n1, e1_q = call(
        functools.partial(first_finish_kernel, peers), [SMEM] + [ANY] * 19, [ANY] * 3, [msg, nb, hb],
        [vmem(x) for x in args] + [wts(4), tmp, vmem(msg), vmem(nb), vmem(hb), DMA(4), DMA(11), DMA(3)],
        10**9, 4 * 10**6,
    )(sec, *args, *own_w, *oth_w)
    halo = halo_exchange(rows)

    args = (n1, e1_q, e1_loc, oh_q, perm_q)
    pre_q, part, pre_n, e1_h, out_l, e_out = call(
        second_local_kernel, [SMEM, SMEM] + [ANY] * 15, [ANY] * 6, [hf, nf, nf, hb, hb, outs[1]],
        [vmem(x) for x in (src, dst, vec, vec) + args] + [wts(5)] + [vmem(x) for x in (hf, nf, nf, hb, hb, hb)]
        + [DMA(5), DMA(9), DMA(6)],
        2 * 10**9, 10**7,
    )(sec, edge_count, src, dst, *args, *own_w[:3], *oth_w[:3], vec, oth_vec)
    oth_l = swap(out_l)

    args = (halo, pre_q, vec, oth_vec, live_q, oh_q, part, e1_q, pre_n, n1, perm_q, e1_h, oth_l)
    cross, n_out, e_out = call(
        functools.partial(last_finish_kernel, peers), [SMEM] + [ANY] * 22, [ANY] * 3,
        [shape((nodes + half, width), BF16)] + outs,
        [vmem(x) for x in args] + [wts(4), tmp, vmem(hb), vmem(hb), vmem(nb), vmem(nb), DMA(4), DMA(13), DMA(5)],
        10**9, 4 * 10**6, input_output_aliases={22: 2},
    )(sec, *args, *own_w, *oth_w, e_out)
    crossed = swap(cross)

    return call(other_out_kernel, [SMEM, VMEM, ANY, ANY], [ANY, ANY], outs, [DMA(2)], 0, 3 * 10**6,
                limit=1024 * 1024, input_output_aliases={2: 0, 3: 1})(sec, crossed, n_out, e_out)


def solution(mesh):
    in_specs = (
        P(None, "dom", None),
        P(None, "dom", None),
        P("dom"),
        P("dom"),
        P("dom"),
        P("dom", None),
        P("section", None, None, None),
        P("section", None),
        P("section", None, None),
        P("section", None),
        P("section", None, None, None),
        P("section", None),
        P("section", None, None),
        P("section", None),
    )
    out_specs = (P("section", None, "dom", None), P("section", None, "dom", None))
    return jax.shard_map(layers, mesh=mesh, in_specs=in_specs, out_specs=out_specs, check_vma=False)
```
